32 devices in a mesh: step: 2 (over core), tile: 16 (over z, y, x).
Axes of the slice: x: 2, y: 2, z: 4, core: 2. Of those that a mesh axis runs over, the one named last changes fastest.
Arguments:
- latents: float32 [2, 2048, 3072], P('step', 'tile'), may hold values from -6 to 6
- start: float32 [2048, 3072], P('tile'), may hold values from -6 to 6
- cached_velocity: float32 [2, 2048, 3072], P('step', 'tile'), may hold values from -4 to 4
- shift: float32 [2, 3072], P('step'), may hold values from -3 to 3
- scale: float32 [2, 3072], P('step'), may hold values from -3 to 3
- gate: float32 [2, 3072], P('step'), may hold values from -10 to 10
- step_sizes: float32 [2], P('step'), may hold values from 0.1 to 0.5
- converged: int32 [2, 16], P(None, 'tile'), may hold values from 0 to 1, as said below
- neighbours: int32 [16, 4], P('tile'), may hold values from 0 to 1, as said below
- w_qkv: bfloat16 [3, 3072, 2048], P(None, None, 'step'), may hold values from -0.109375 to 0.109375
- q_gain: float32 [128], replicated, may hold values from 0.1 to 1.9
- k_gain: float32 [128], replicated, may hold values from 0.1 to 1.9
- w_out: bfloat16 [2048, 3072], P('step', 'tile'), may hold values from -0.5 to 0.5
Outputs:
- updated: float32 [2, 2048, 3072], P('step', 'tile')
- velocity: float32 [2, 2048, 3072], P('step', 'tile')
The draws below stay inside these ranges and needn't reach their ends.
Inputs may be any that keep to these rules, and one draw needn't show every extreme that they name: For each tile the converged steps are the first ones of the window, at most 1 of them. `neighbours`: an entry is 0 wherever the grid of 4 rows of 4 tiles has no neighbour that way.
All inputs are finite; a program needn't handle non-finite values.
Results may differ from the reference program's by a relative error of at most 0.008.
Values may be sent and summed in bfloat16 or wider, within the bound.
A program may use at most 128 MiB of HBM per device.

```python
import math
import jax
import jax.numpy as jnp
from jax import lax

D = 3072
HEADS = 16
HD = 128
GRID_COLS = 4
TILE_TOK = 128
STEPS = 2
TOKENS = 2048
N_TILE = 16


def draw_converged(key, part):
    counts = jax.random.randint(key, (N_TILE,), 0, STEPS // 2 + 1)
    positions = jnp.arange(STEPS)[:, None]
    return (positions < counts[None, :]).astype(jnp.int32)


def draw_neighbours(key, part):
    picks = jax.random.randint(key, (N_TILE, 4), 0, 4) > 0
    tiles = jnp.arange(N_TILE)
    column = tiles % GRID_COLS
    row_index = tiles // GRID_COLS
    row_count = N_TILE // GRID_COLS
    valid = jnp.stack([column > 0, column < GRID_COLS - 1, row_index > 0, row_index < row_count - 1], axis=1)
    return (picks & valid).astype(jnp.int32)


def shard_levels(stream_key, shape, pieces, low, top_value):
    level, own = 1.0, jax.random.fold_in(stream_key, 6)
    for dim, shards_of in pieces:
        draws = jnp.exp(jax.random.uniform(jax.random.fold_in(own, dim), (shards_of,), jnp.float32, low / len(pieces), top_value / len(pieces)))
        level = level * jnp.repeat(draws, shape[dim] // shards_of).reshape([-1 if axis == dim else 1 for axis in range(len(shape))])
    return level


def centred(stream_key, dims, scale, reach, split=(), held_as=jnp.bfloat16):
    factor_of = shard_levels(stream_key, dims, split, -0.22, 0.18) if split else 1.0
    result = jax.random.normal(stream_key, dims, jnp.float32) * scale * factor_of
    return jnp.minimum(jnp.maximum(result, -reach), reach).astype(held_as)


def setup_inputs(seed: int = 0) -> dict:
    keys = jax.random.split(jax.random.key(seed), 14)
    return {
        "latents": centred(keys[0], (STEPS, TOKENS, D), 1.0, 6.0, ((0, 2), (1, 16)), jnp.float32),
        "start": centred(keys[1], (TOKENS, D), 1.0, 6.0, ((0, 16),), jnp.float32),
        "cached_velocity": centred(keys[2], (STEPS, TOKENS, D), 0.5, 4.0, ((0, 2), (1, 16)), jnp.float32),
        "shift": centred(keys[3], (STEPS, D), 0.5, 3.0, ((0, 2),), jnp.float32),
        "scale": centred(keys[4], (STEPS, D), 0.5, 3.0, ((0, 2),), jnp.float32),
        "gate": centred(keys[5], (STEPS, D), 2.0, 10.0, ((0, 2),), jnp.float32),
        "step_sizes": jnp.clip(jnp.exp(math.log(0.5) - 1.609438 * jax.random.uniform(keys[6], (STEPS,), jnp.float32) ** shard_levels(keys[6], (STEPS,), ((0, 2),), -0.2, 0.2)), 0.1, 0.5),
        "converged": draw_converged(jax.random.fold_in(keys[13], 71), 0),
        "neighbours": draw_neighbours(jax.random.fold_in(keys[13], 71), 0),
        "w_qkv": centred(keys[9], (3, D, HEADS * HD), D ** -0.5, 0.109375, ((2, 2),)),
        "q_gain": jnp.clip(1.0 + 0.18 * jax.random.normal(keys[10], (HD,), jnp.float32), 0.1, 1.9),
        "k_gain": jnp.clip(1.0 + 0.18 * jax.random.normal(keys[11], (HD,), jnp.float32), 0.1, 1.9),
        "w_out": centred(keys[12], (HEADS * HD, D), HD ** -0.5, 0.5, ((0, 2), (1, 16))),
    }


def reference(latents, start, cached_velocity, shift, scale, gate, step_sizes, converged, neighbours, w_qkv, q_gain, k_gain, w_out):
    high = lax.Precision.HIGHEST
    key_mask = jnp.concatenate([jnp.ones((N_TILE, TILE_TOK), jnp.float32), jnp.repeat(neighbours.astype(jnp.float32), TILE_TOK, axis=1)], axis=1)
    weights_f = w_qkv.astype(jnp.float32)
    out_f = w_out.astype(jnp.float32)

    def one_step(items):
        lat, shf, scl = items
        mean = lax.optimization_barrier(jnp.mean(lat, axis=-1, keepdims=True))
        var = lax.optimization_barrier(jnp.mean(jnp.square(lat - mean), axis=-1, keepdims=True))
        normed = ((lat - mean) / jnp.sqrt(var + 1e-06) * (1.0 + scl) + shf).astype(jnp.bfloat16)
        qkv = jnp.einsum('td,cdf->ctf', normed.astype(jnp.float32), weights_f, precision=high)
        qkv = qkv.reshape(3, N_TILE, TILE_TOK, HEADS, HD)

        def rms(block, gain):
            return (block / jnp.sqrt(lax.optimization_barrier(jnp.mean(block * block, axis=-1, keepdims=True)) + 1e-06) * gain).astype(jnp.bfloat16)
        queries = rms(qkv[0], q_gain)
        keys_own = rms(qkv[1], k_gain)
        values_own = qkv[2].astype(jnp.bfloat16)

        def beside_all(block):
            return jnp.concatenate([block, jnp.roll(block, 1, axis=0), jnp.roll(block, -1, axis=0), jnp.roll(block, GRID_COLS, axis=0), jnp.roll(block, -GRID_COLS, axis=0)], axis=1)
        keys_all = beside_all(keys_own).astype(jnp.float32)
        values_all = beside_all(values_own).astype(jnp.float32)
        scores = jnp.einsum('tqhd,tkhd->thqk', queries.astype(jnp.float32), keys_all, precision=high) / jnp.sqrt(jnp.float32(HD))
        expo = jnp.exp(scores) * key_mask[:, None, None, :]
        probs = (expo / lax.optimization_barrier(jnp.sum(expo, axis=-1, keepdims=True))).astype(jnp.bfloat16)
        attended = jnp.einsum('thqk,tkhd->tqhd', probs.astype(jnp.float32), values_all, precision=high).astype(jnp.bfloat16)
        attended = attended.reshape(TOKENS, HEADS * HD)
        return jnp.dot(attended.astype(jnp.float32), out_f, precision=high)
    projected = lax.map(one_step, (latents, shift[:, None, :], scale[:, None, :]))
    frozen = jnp.repeat(converged, TILE_TOK, axis=1)[:, :, None] == 1
    velocity = jnp.where(frozen, cached_velocity, gate[:, None, :] * projected)
    terms = step_sizes[:, None, None] * velocity
    summed = jnp.cumsum(terms, axis=0)
    prefix = jnp.concatenate([jnp.zeros((1, TOKENS, D), jnp.float32), summed[:-1]], axis=0)
    updated = start[None, :, :] + prefix
    return (updated, velocity)
```

```python
import functools
import jax
import jax.numpy as jnp
from jax import lax
from jax.experimental import pallas as pl
from jax.experimental.pallas import tpu as pltpu
from jax.sharding import PartitionSpec as P

GRID_COLS = 4
MESH = pl.DeviceIdType.MESH
BF16 = jnp.bfloat16
F32 = jnp.float32


def nearest(place, length):
    if length == 1:
        return [place]
    if length == 2:
        return [place, 1 - place]
    assert length == 4
    inner = (place * (3 - place)) // 2
    flip, turn = 3 - place, lax.rem(place + 2, 4)
    beside = place + 1 - 2 * lax.rem(place, 2)
    return [
        place,
        beside,
        inner * flip + (1 - inner) * turn,
        inner * turn + (1 - inner) * flip,
    ]


def kernel(
    tiles,
    dims,
    lat_ref,
    start_ref,
    cached_ref,
    shift_ref,
    scale_ref,
    gate_ref,
    sizes_ref,
    conv_ref,
    near_ref,
    wqkv_ref,
    qg_ref,
    kg_ref,
    wt_ref,
    upd_ref,
    vel_ref,
    nbuf,
    wbuf,
    kvbuf,
    qbuf,
    abuf,
    gbuf,
    cbuf,
    sbuf,
    pbuf,
    xsend,
    xrecv,
    ssend,
    srecv,
    vbuf,
    ubuf,
    w_sem,
    in_sem,
    n_sem,
    kv_send,
    kv_recv,
    g_send,
    g_recv,
    x_sem,
    s_sem,
    out_sem,
):
    lz, ly, lx = dims
    s = lax.axis_index("step")
    t = lax.axis_index("tile")
    other = 1 - s
    zc, yc, xc = t // (ly * lx), lax.rem(t // lx, ly), lax.rem(t, lx)
    col, row = lax.rem(t, GRID_COLS), t // GRID_COLS
    rows = tiles // GRID_COLS
    tok, width = lat_ref.shape[1], lat_ref.shape[2]
    chunks, cw = kvbuf.shape[1], kvbuf.shape[4]
    hd = qg_ref.shape[1]
    heads = cw // hd
    relay = lx == 2 and ly == 2 and GRID_COLS == 4
    planes = lz
    pcols = width // planes

    strides = (ly * lx, lx, 1)
    coords = (zc, yc, xc)
    barrier = pltpu.get_barrier_semaphore()
    links = []
    for d in range(3):
        covered = strides[d] == GRID_COLS or (strides[d] == 1 and not relay)
        if dims[d] > 1 and not covered:
            links.append((coords[d] < dims[d] - 1, t + strides[d]))
            links.append((coords[d] > 0, t - strides[d]))
    if not relay:
        links.append((col < GRID_COLS - 1, t + 1))
        links.append((col > 0, t - 1))
    links.append((row < rows - 1, t + GRID_COLS))
    links.append((row > 0, t - GRID_COLS))
    pl.semaphore_signal(barrier, inc=1, device_id={"step": other}, device_id_type=MESH)
    for valid, peer in links:

        @pl.when(valid)
        def _(peer=peer):
            pl.semaphore_signal(barrier, inc=1, device_id={"tile": peer}, device_id_type=MESH)

    def w_copy(i):
        return pltpu.make_async_copy(
            wqkv_ref.at[i % 3, :, pl.ds((i // 3) * cw, cw)], wbuf.at[i % 3, i // 3], w_sem.at[i]
        )

    for c in range(chunks):
        w_copy(3 * c + 1).start()
        w_copy(3 * c + 2).start()
    for c in range(chunks):
        w_copy(3 * c).start()
    hw = gbuf.shape[3]
    own_w = [
        pltpu.make_async_copy(wt_ref.at[:, pl.ds(h * hw, hw)], gbuf.at[h, t], in_sem.at[h])
        for h in range(2)
    ]
    for copy in own_w:
        copy.start()
    cached_copy = pltpu.make_async_copy(cached_ref.at[0], cbuf, in_sem.at[2])
    start_copy = pltpu.make_async_copy(start_ref, sbuf, in_sem.at[3])
    cached_copy.start()
    start_copy.start()

    pl.semaphore_wait(barrier, 1 + sum(valid.astype(jnp.int32) for valid, _ in links))

    orders = ((0, 1, 2), (0, 2, 1))
    lines = [nearest(coords[d], dims[d]) for d in range(3)]

    def g_copy(h, source, src, d, up):
        peer = t + strides[d] if up else t - strides[d]
        return pltpu.make_async_remote_copy(
            src_ref=src,
            dst_ref=gbuf.at[h, source],
            send_sem=g_send.at[h, source, 2 * d + (1 if up else 0)],
            recv_sem=g_recv.at[h, source],
            device_id={"tile": peer},
            device_id_type=MESH,
        )

    def g_each(offset, act):
        source = sum(lines[d][offset[d]] * strides[d] for d in range(3))
        for h in range(2):
            order = orders[h]
            for j in range(3):
                d = order[j]
                if any(offset[e] != 0 for e in order[j + 1 :]):
                    continue
                for up in (True, False):
                    if up:
                        valid = coords[d] < dims[d] - 1
                    else:
                        valid = coords[d] > 0
                    if offset[d] != 0:
                        if dims[d] == 2:
                            continue
                        place = lines[d][offset[d]]
                        away = coords[d] > place if up else coords[d] < place
                        valid = jnp.logical_and(valid, away)

                    @pl.when(valid)
                    def _(h=h, d=d, up=up):
                        own = offset == (0, 0, 0)
                        src = wt_ref.at[:, pl.ds(h * hw, hw)] if own else gbuf.at[h, source]
                        act(g_copy(h, source, src, d, up))

    def g_step(offset):
        if offset != (0, 0, 0):
            source = sum(lines[d][offset[d]] * strides[d] for d in range(3))
            for h in range(2):
                pltpu.make_async_remote_copy(
                    src_ref=gbuf.at[h, source],
                    dst_ref=gbuf.at[h, source],
                    send_sem=g_send.at[h, source, 0],
                    recv_sem=g_recv.at[h, source],
                    device_id={"step": other},
                    device_id_type=MESH,
                ).wait_recv()
        g_each(offset, lambda copy: copy.start())

    offsets = [
        (a, b, c)
        for a in range(dims[0])
        for b, c in sorted(
            [(b, c) for b in range(dims[1]) for c in range(dims[2])], key=lambda v: v[0] + v[1]
        )
    ]
    g_step((0, 0, 0))

    def n_copy(part):
        half = tok // 2
        where = nbuf.at[s, pl.ds(part * half, half)]
        return pltpu.make_async_remote_copy(
            src_ref=where,
            dst_ref=where,
            send_sem=n_sem.at[0, part],
            recv_sem=n_sem.at[1, part],
            device_id={"step": other},
            device_id_type=MESH,
        )

    for part in range(2):
        half = tok // 2
        own = lat_ref[0, pl.ds(part * half, half), :]
        mean = jnp.mean(own, axis=-1, keepdims=True)
        cent = own - mean
        var = jnp.mean(cent * cent, axis=-1, keepdims=True)
        normed = cent / jnp.sqrt(var + 1e-06) * (1.0 + scale_ref[...]) + shift_ref[...]
        nbuf[s, pl.ds(part * half, half), :] = normed.astype(BF16)
        n_copy(part).start()

    present = (None, col > 0, col < GRID_COLS - 1, row > 0, row < rows - 1)
    for j in range(1, 5):

        @pl.when(jnp.logical_not(present[j]))
        def _(j=j):
            @pl.loop(0, chunks)
            def _(c):
                kvbuf[j, c] = jnp.zeros(kvbuf.shape[2:], BF16)

    for part in range(2):
        n_copy(part).wait()

    def kv_copy(src_slot, slot, sem, c, peer):
        return pltpu.make_async_remote_copy(
            src_ref=kvbuf.at[src_slot, c],
            dst_ref=kvbuf.at[slot, c],
            send_sem=kv_send.at[sem, c],
            recv_sem=kv_recv.at[slot, c],
            device_id={"tile": peer},
            device_id_type=MESH,
        )

    right, left = col < GRID_COLS - 1, col > 0
    if relay:
        right, left = lax.rem(col, 2) == 0, lax.rem(col, 2) == 1
    sends = (
        (1, right, t + 1),
        (2, left, t - 1),
        (3, row < rows - 1, t + GRID_COLS),
        (4, row > 0, t - GRID_COLS),
    )

    def kv_sends(c, act):
        for slot, valid, peer in sends:

            @pl.when(valid)
            def _(slot=slot, peer=peer):
                act(kv_copy(0, slot, slot, c, peer))

    passed = ((2, 1, col == 0, t + 2), (1, 2, col == 3, t - 2))

    def kv_wait(c, slots):
        for slot in slots:

            @pl.when(present[slot])
            def _(slot=slot):
                pltpu.make_async_remote_copy(
                    src_ref=kvbuf.at[slot, c],
                    dst_ref=kvbuf.at[slot, c],
                    send_sem=kv_send.at[slot, c],
                    recv_sem=kv_recv.at[slot, c],
                    device_id={"step": other},
                    device_id_type=MESH,
                ).wait_recv()

    def kv_pass(c):
        if not relay:
            return
        for slot, onward, valid, peer in passed:

            @pl.when(lax.rem(col, 2) == (0 if slot == 2 else 1))
            def _(slot=slot):
                pltpu.make_async_remote_copy(
                    src_ref=kvbuf.at[slot, c],
                    dst_ref=kvbuf.at[slot, c],
                    send_sem=kv_send.at[slot, c],
                    recv_sem=kv_recv.at[slot, c],
                    device_id={"step": other},
                    device_id_type=MESH,
                ).wait_recv()

            @pl.when(valid)
            def _(slot=slot, onward=onward, peer=peer):
                kv_copy(slot, onward, 0, c, peer).start()

    def kv_rest(c):
        if not relay:
            kv_wait(c, (1, 2, 3, 4))
            return
        for slot, valid in ((1, col == 2), (2, col == 1)):

            @pl.when(valid)
            def _(slot=slot):
                pltpu.make_async_remote_copy(
                    src_ref=kvbuf.at[slot, c],
                    dst_ref=kvbuf.at[slot, c],
                    send_sem=kv_send.at[slot, c],
                    recv_sem=kv_recv.at[slot, c],
                    device_id={"step": other},
                    device_id_type=MESH,
                ).wait_recv()

        kv_wait(c, (3, 4))

    def project(which, c):
        block = nbuf[...].reshape(2 * tok, width)
        return jnp.dot(block, wbuf[which, c], preferred_element_type=F32)

    def rms(result, gain):
        parts = []
        for h in range(heads):
            part = result[:, h * hd : (h + 1) * hd]
            square = jnp.mean(part * part, axis=-1, keepdims=True)
            parts.append(part / jnp.sqrt(square + 1e-06) * gain)
        return jnp.concatenate(parts, axis=-1).astype(BF16)

    def w_wait(which, c):
        pltpu.make_async_copy(
            wqkv_ref.at[which, :, pl.ds(0, cw)], wbuf.at[which, c], w_sem.at[3 * c + which]
        ).wait()

    @pl.loop(0, chunks)
    def _(c):
        w_wait(1, c)
        kvbuf[0, c, 0] = rms(project(1, c), kg_ref[...])
        w_wait(2, c)
        kvbuf[0, c, 1] = project(2, c).astype(BF16)
        kv_sends(c, lambda copy: copy.start())

    for offset in offsets[1 : ly * lx]:
        g_step(offset)

    @pl.loop(0, chunks)
    def _(c):
        w_wait(0, c)
        qbuf[c] = rms(project(0, c), qg_ref[...])

    factor = 1.0 / jnp.sqrt(jnp.float32(hd))
    ones = jnp.ones((1, tok), F32)
    mask = jnp.concatenate(
        [ones] + [ones * near_ref[0, j].astype(F32) for j in range(4)], axis=1
    )
    per_half = abuf.shape[3] // cw

    def attention(c):
        @pl.loop(0, 2)
        def _(k):
            at = pl.ds(pl.multiple_of(k * tok, tok), tok)
            for h in range(heads):
                cols = pl.ds(h * hd, hd)
                q = qbuf[c, at, cols]
                keys = kvbuf[:, c, 0, at, cols].reshape(5 * tok, hd)
                values = kvbuf[:, c, 1, at, cols].reshape(5 * tok, hd)
                scores = lax.dot_general(
                    q, keys, (((1,), (1,)), ((), ())), preferred_element_type=F32
                )
                expo = jnp.exp(scores * factor) * mask
                probs = (expo / jnp.sum(expo, axis=-1, keepdims=True)).astype(BF16)
                out = jnp.dot(probs, values, preferred_element_type=F32)
                abuf[c // per_half, k, :, pl.ds((c % per_half) * cw + h * hd, hd)] = out.astype(
                    BF16
                )

    plane = ly * lx
    later = [g for a in range(1, lz) for g in offsets[a * plane : (a + 1) * plane]]
    todo = list(later)
    kv_pass(0)
    g_step(todo.pop(0))
    kv_pass(1)
    kv_pass(2)
    for offset in [todo.pop(0) for _ in range(min(2, len(todo)))]:
        g_step(offset)
    kv_pass(3) if chunks > 3 else None
    for c in range(4, chunks):
        kv_pass(c)
    for c in range(chunks):
        kv_rest(c)
        attention(c)
        if todo:
            g_step(todo.pop(0))

    for copy in own_w:
        copy.wait()
    cached_copy.wait()
    start_copy.wait()
    flag = conv_ref[s, 0] > 0

    def x_copy(k):
        return pltpu.make_async_remote_copy(
            src_ref=xsend.at[k],
            dst_ref=xrecv.at[k],
            send_sem=x_sem.at[0, k],
            recv_sem=x_sem.at[1, k],
            device_id={"step": other},
            device_id_type=MESH,
        )

    def s_copy(k):
        return pltpu.make_async_remote_copy(
            src_ref=ssend.at[k],
            dst_ref=srecv.at[k],
            send_sem=s_sem.at[0, k],
            recv_sem=s_sem.at[1, k],
            device_id={"step": other},
            device_id_type=MESH,
        )

    def at_cols(k):
        return pl.ds(pl.multiple_of(lines[0][k] * pcols, 128), pcols)

    def out_copy(k, which):
        src, dst = ((ubuf, upd_ref), (vbuf, vel_ref))[which]
        return pltpu.make_async_copy(src.at[k], dst.at[0, :, at_cols(k)], out_sem.at[which, k])

    def out_dot(k):
        which = pl.ds(lines[0][k] * plane, plane)
        total = None
        for h in range(2):
            weights = gbuf[h, which].reshape(pcols, gbuf.shape[3])
            block = abuf[h].reshape(2 * tok, gbuf.shape[3])
            term = lax.dot_general(
                block, weights, (((1,), (1,)), ((), ())), preferred_element_type=F32
            )
            total = term if total is None else total + term
        pbuf[k] = total.reshape(2, tok, pcols)
        xsend[k] = pbuf[k, other].astype(BF16)
        x_copy(k).start()

    def finish(k):
        x_copy(k).wait()
        projected = pbuf[k, s] + xrecv[k].astype(F32)
        velocity = jnp.where(flag, cbuf[:, at_cols(k)], gate_ref[:, at_cols(k)] * projected)
        vbuf[k] = velocity
        out_copy(k, 1).start()

        @pl.when(s == 0)
        def _():
            ssend[k] = (sizes_ref[0] * velocity).astype(BF16)
            s_copy(k).start()
            ubuf[k] = sbuf[:, at_cols(k)]
            out_copy(k, 0).start()

    def finish_later(k):
        @pl.when(s == 1)
        def _():
            s_copy(k).wait_recv()
            ubuf[k] = sbuf[:, at_cols(k)] + srecv[k].astype(F32)
            out_copy(k, 0).start()

    for k in range(planes):
        while len(todo) > (planes - 1 - k) * plane:
            g_step(todo.pop(0))
        out_dot(k)
        if k >= 1:
            finish(k - 1)
        if k >= 2:
            finish_later(k - 2)
    finish(planes - 1)
    if planes >= 2:
        finish_later(planes - 2)
    finish_later(planes - 1)

    for offset in offsets:
        g_each(offset, lambda copy: copy.wait_send())

    @pl.loop(0, chunks)
    def _(c):
        kv_sends(c, lambda copy: copy.wait_send())
        if relay:
            for slot, onward, valid, peer in passed:

                @pl.when(valid)
                def _(slot=slot, onward=onward, peer=peer):
                    kv_copy(slot, onward, 0, c, peer).wait_send()

    @pl.when(s == 0)
    def _():
        for k in range(planes):
            s_copy(k).wait_send()

    for k in range(planes):
        out_copy(k, 0).wait()
        out_copy(k, 1).wait()


def split(tiles):
    side = int(round((tiles // 4) ** 0.5))
    assert 4 * side * side == tiles
    return (4, side, side)


def body(tiles, *args):
    (
        latents,
        start,
        cached_velocity,
        shift,
        scale,
        gate,
        step_sizes,
        converged,
        neighbours,
        w_qkv,
        q_gain,
        k_gain,
        w_out,
    ) = args
    tok, width = latents.shape[1], latents.shape[2]
    group = w_qkv.shape[2]
    hd = q_gain.shape[0]
    shard = w_out.shape[1]
    dims = split(tiles)
    planes = dims[0]
    pcols = width // planes
    cw = 2 * hd
    chunks = group // cw
    wt = w_out.T
    any_space = pl.BlockSpec(memory_space=pl.ANY)
    vmem = pl.BlockSpec(memory_space=pltpu.VMEM)
    smem = pl.BlockSpec(memory_space=pltpu.SMEM)
    dma = pltpu.SemaphoreType.DMA
    upd, vel = pl.pallas_call(
        functools.partial(kernel, tiles, dims),
        out_shape=[jax.ShapeDtypeStruct((1, tok, width), F32)] * 2,
        in_specs=[
            vmem,
            any_space,
            any_space,
            vmem,
            vmem,
            vmem,
            smem,
            smem,
            smem,
            any_space,
            vmem,
            vmem,
            any_space,
        ],
        out_specs=[any_space, any_space],
        scratch_shapes=[
            pltpu.VMEM((2, tok, width), BF16),
            pltpu.VMEM((3, chunks, width, cw), BF16),
            pltpu.VMEM((5, chunks, 2, 2 * tok, cw), BF16),
            pltpu.VMEM((chunks, 2 * tok, cw), BF16),
            pltpu.VMEM((2, 2, tok, group // 2), BF16),
            pltpu.VMEM((2, tiles, shard, group // 2), BF16),
            pltpu.VMEM((tok, width), F32),
            pltpu.VMEM((tok, width), F32),
            pltpu.VMEM((planes, 2, tok, pcols), F32),
            pltpu.VMEM((planes, tok, pcols), BF16),
            pltpu.VMEM((planes, tok, pcols), BF16),
            pltpu.VMEM((planes, tok, pcols), BF16),
            pltpu.VMEM((planes, tok, pcols), BF16),
            pltpu.VMEM((planes, tok, pcols), F32),
            pltpu.VMEM((planes, tok, pcols), F32),
            dma((3 * chunks,)),
            dma((4,)),
            dma((2, 2)),
            dma((5, chunks)),
            dma((5, chunks)),
            dma((2, tiles, 6)),
            dma((2, tiles)),
            dma((2, planes)),
            dma((2, planes)),
            dma((2, planes)),
        ],
        compiler_params=pltpu.CompilerParams(
            collective_id=0, has_side_effects=True, vmem_limit_bytes=60 * 1024 * 1024
        ),
    )(
        latents,
        start,
        cached_velocity,
        shift,
        scale,
        gate,
        step_sizes,
        converged,
        neighbours,
        w_qkv,
        q_gain[None],
        k_gain[None],
        wt,
    )
    return (upd, vel)


def solution(mesh):
    assert mesh.shape["step"] == 2
    placed = (
        P("step", "tile", None),
        P("tile", None),
        P("step", "tile", None),
        P("step", None),
        P("step", None),
        P("step", None),
        P("step"),
        P(None, "tile"),
        P("tile", None),
        P(None, None, "step"),
        P(),
        P(),
        P("step", "tile"),
    )
    return jax.shard_map(
        functools.partial(body, mesh.shape["tile"]),
        mesh=mesh,
        in_specs=placed,
        out_specs=(P("step", "tile", None), P("step", "tile", None)),
        check_vma=False,
    )
```

```python
import functools
import jax
import jax.numpy as jnp
from jax import lax
from jax.experimental import pallas as pl
from jax.experimental.pallas import tpu as pltpu
from jax.sharding import PartitionSpec as P

GRID_COLS = 4
MESH = pl.DeviceIdType.MESH
BF16 = jnp.bfloat16
F32 = jnp.float32


def nearest(place, length):
    if length == 1:
        return [place]
    if length == 2:
        return [place, 1 - place]
    assert length == 4
    inner = (place * (3 - place)) // 2
    flip, turn = 3 - place, lax.rem(place + 2, 4)
    beside = place + 1 - 2 * lax.rem(place, 2)
    return [
        place,
        beside,
        inner * flip + (1 - inner) * turn,
        inner * turn + (1 - inner) * flip,
    ]


def kernel(
    tiles,
    dims,
    lat_ref,
    start_ref,
    cached_ref,
    shift_ref,
    scale_ref,
    gate_ref,
    sizes_ref,
    conv_ref,
    near_ref,
    wqkv_ref,
    qg_ref,
    kg_ref,
    wt_ref,
    upd_ref,
    vel_ref,
    nbuf,
    wbuf,
    kvbuf,
    qbuf,
    abuf,
    apeer,
    gbuf,
    cbuf,
    sbuf,
    pbuf,
    xsend,
    xrecv,
    ssend,
    srecv,
    ysend,
    yrecv,
    vbuf,
    ubuf,
    w_sem,
    in_sem,
    n_sem,
    kv_send,
    kv_recv,
    g_send,
    g_recv,
    x_sem,
    s_sem,
    a_sem,
    y_sem,
    out_sem,
):
    lz, ly, lx = dims
    s = lax.axis_index("step")
    t = lax.axis_index("tile")
    other = 1 - s
    zc, yc, xc = t // (ly * lx), lax.rem(t // lx, ly), lax.rem(t, lx)
    col, row = lax.rem(t, GRID_COLS), t // GRID_COLS
    rows = tiles // GRID_COLS
    tok, width = lat_ref.shape[1], lat_ref.shape[2]
    chunks, cw = kvbuf.shape[1], kvbuf.shape[4]
    hd = qg_ref.shape[1]
    heads = cw // hd
    relay = lx == 2 and ly == 2 and GRID_COLS == 4
    pair = ly == 2
    planes = lz
    groups = 2 if pair else 1
    pcols = width // planes // groups
    plane = lx if pair else ly * lx

    strides = (ly * lx, lx, 1)
    coords = (zc, yc, xc)
    barrier = pltpu.get_barrier_semaphore()
    links = []
    for d in range(3):
        covered = strides[d] == GRID_COLS or (strides[d] == 1 and not relay)
        if dims[d] > 1 and not covered:
            links.append((coords[d] < dims[d] - 1, t + strides[d]))
            links.append((coords[d] > 0, t - strides[d]))
    if not relay:
        links.append((col < GRID_COLS - 1, t + 1))
        links.append((col > 0, t - 1))
    links.append((row < rows - 1, t + GRID_COLS))
    links.append((row > 0, t - GRID_COLS))
    pl.semaphore_signal(barrier, inc=1, device_id={"step": other}, device_id_type=MESH)
    for valid, peer in links:

        @pl.when(valid)
        def _(peer=peer):
            pl.semaphore_signal(barrier, inc=1, device_id={"tile": peer}, device_id_type=MESH)

    def w_copy(i):
        return pltpu.make_async_copy(
            wqkv_ref.at[i % 3, :, pl.ds((i // 3) * cw, cw)], wbuf.at[i % 3, i // 3], w_sem.at[i]
        )

    for c in range(chunks):
        w_copy(3 * c + 1).start()
        w_copy(3 * c + 2).start()
    for c in range(chunks):
        w_copy(3 * c).start()
    hw = gbuf.shape[3]

    def spot(tile):
        return (tile // (ly * lx)) * lx + lax.rem(tile, lx) if pair else tile

    own_w = [
        pltpu.make_async_copy(wt_ref.at[:, pl.ds(h * hw, hw)], gbuf.at[h, spot(t)], in_sem.at[h])
        for h in range(2)
    ]
    for copy in own_w:
        copy.start()
    cached_copy = pltpu.make_async_copy(cached_ref.at[0], cbuf, in_sem.at[2])
    start_copy = pltpu.make_async_copy(start_ref, sbuf, in_sem.at[3])
    cached_copy.start()
    start_copy.start()

    pl.semaphore_wait(barrier, 1 + sum(valid.astype(jnp.int32) for valid, _ in links))

    orders = ((0, 2), (0, 2)) if pair else ((0, 1, 2), (0, 2, 1))
    lines = [nearest(coords[d], dims[d]) for d in range(3)]

    def g_copy(h, source, src, d, up):
        peer = t + strides[d] if up else t - strides[d]
        return pltpu.make_async_remote_copy(
            src_ref=src,
            dst_ref=gbuf.at[h, spot(source)],
            send_sem=g_send.at[h, spot(source), 2 * d + (1 if up else 0)],
            recv_sem=g_recv.at[h, spot(source)],
            device_id={"tile": peer},
            device_id_type=MESH,
        )

    def g_each(offset, act):
        source = sum(lines[d][offset[d]] * strides[d] for d in range(3))
        for h in range(2):
            order = orders[h]
            for j in range(len(order)):
                d = order[j]
                if any(offset[e] != 0 for e in order[j + 1 :]):
                    continue
                for up in (True, False):
                    if up:
                        valid = coords[d] < dims[d] - 1
                    else:
                        valid = coords[d] > 0
                    if offset[d] != 0:
                        if dims[d] == 2:
                            continue
                        place = lines[d][offset[d]]
                        away = coords[d] > place if up else coords[d] < place
                        valid = jnp.logical_and(valid, away)

                    @pl.when(valid)
                    def _(h=h, d=d, up=up):
                        own = offset == (0, 0, 0)
                        src = wt_ref.at[:, pl.ds(h * hw, hw)] if own else gbuf.at[h, spot(source)]
                        act(g_copy(h, source, src, d, up))

    def g_step(offset):
        if offset != (0, 0, 0):
            source = sum(lines[d][offset[d]] * strides[d] for d in range(3))
            for h in range(2):
                pltpu.make_async_remote_copy(
                    src_ref=gbuf.at[h, spot(source)],
                    dst_ref=gbuf.at[h, spot(source)],
                    send_sem=g_send.at[h, spot(source), 0],
                    recv_sem=g_recv.at[h, spot(source)],
                    device_id={"step": other},
                    device_id_type=MESH,
                ).wait_recv()
        g_each(offset, lambda copy: copy.start())

    offsets = [
        (a, b, c)
        for a in range(dims[0])
        for b, c in sorted(
            [(b, c) for b in range(1 if pair else dims[1]) for c in range(dims[2])], key=lambda v: v[0] + v[1]
        )
    ]
    g_step((0, 0, 0))

    def n_copy(part):
        half = tok // 2
        where = nbuf.at[s, pl.ds(part * half, half)]
        return pltpu.make_async_remote_copy(
            src_ref=where,
            dst_ref=where,
            send_sem=n_sem.at[0, part],
            recv_sem=n_sem.at[1, part],
            device_id={"step": other},
            device_id_type=MESH,
        )

    for part in range(2):
        half = tok // 2
        own = lat_ref[0, pl.ds(part * half, half), :]
        mean = jnp.mean(own, axis=-1, keepdims=True)
        cent = own - mean
        var = jnp.mean(cent * cent, axis=-1, keepdims=True)
        normed = cent / jnp.sqrt(var + 1e-06) * (1.0 + scale_ref[...]) + shift_ref[...]
        nbuf[s, pl.ds(part * half, half), :] = normed.astype(BF16)
        n_copy(part).start()

    present = (None, col > 0, col < GRID_COLS - 1, row > 0, row < rows - 1)
    for j in range(1, 5):

        @pl.when(jnp.logical_not(present[j]))
        def _(j=j):
            @pl.loop(0, chunks)
            def _(c):
                kvbuf[j, c] = jnp.zeros(kvbuf.shape[2:], BF16)

    for part in range(2):
        n_copy(part).wait()

    def kv_copy(src_slot, slot, sem, c, peer):
        return pltpu.make_async_remote_copy(
            src_ref=kvbuf.at[src_slot, c],
            dst_ref=kvbuf.at[slot, c],
            send_sem=kv_send.at[sem, c],
            recv_sem=kv_recv.at[slot, c],
            device_id={"tile": peer},
            device_id_type=MESH,
        )

    right, left = col < GRID_COLS - 1, col > 0
    if relay:
        right, left = lax.rem(col, 2) == 0, lax.rem(col, 2) == 1
    sends = (
        (1, right, t + 1),
        (2, left, t - 1),
        (3, row < rows - 1, t + GRID_COLS),
        (4, row > 0, t - GRID_COLS),
    )

    def kv_sends(c, act):
        for slot, valid, peer in sends:

            @pl.when(valid)
            def _(slot=slot, peer=peer):
                act(kv_copy(0, slot, slot, c, peer))

    passed = ((2, 1, col == 0, t + 2), (1, 2, col == 3, t - 2))

    def kv_wait(c, slots):
        for slot in slots:

            @pl.when(present[slot])
            def _(slot=slot):
                pltpu.make_async_remote_copy(
                    src_ref=kvbuf.at[slot, c],
                    dst_ref=kvbuf.at[slot, c],
                    send_sem=kv_send.at[slot, c],
                    recv_sem=kv_recv.at[slot, c],
                    device_id={"step": other},
                    device_id_type=MESH,
                ).wait_recv()

    def kv_pass(c):
        if not relay:
            return
        for slot, onward, valid, peer in passed:

            @pl.when(lax.rem(col, 2) == (0 if slot == 2 else 1))
            def _(slot=slot):
                pltpu.make_async_remote_copy(
                    src_ref=kvbuf.at[slot, c],
                    dst_ref=kvbuf.at[slot, c],
                    send_sem=kv_send.at[slot, c],
                    recv_sem=kv_recv.at[slot, c],
                    device_id={"step": other},
                    device_id_type=MESH,
                ).wait_recv()

            @pl.when(valid)
            def _(slot=slot, onward=onward, peer=peer):
                kv_copy(slot, onward, 0, c, peer).start()

    def kv_rest(c):
        if not relay:
            kv_wait(c, (1, 2, 3, 4))
            return
        for slot, valid in ((1, col == 2), (2, col == 1)):

            @pl.when(valid)
            def _(slot=slot):
                pltpu.make_async_remote_copy(
                    src_ref=kvbuf.at[slot, c],
                    dst_ref=kvbuf.at[slot, c],
                    send_sem=kv_send.at[slot, c],
                    recv_sem=kv_recv.at[slot, c],
                    device_id={"step": other},
                    device_id_type=MESH,
                ).wait_recv()

        kv_wait(c, (3, 4))

    def project(which, c):
        block = nbuf[...].reshape(2 * tok, width)
        return jnp.dot(block, wbuf[which, c], preferred_element_type=F32)

    def rms(result, gain):
        parts = []
        for h in range(heads):
            part = result[:, h * hd : (h + 1) * hd]
            square = jnp.mean(part * part, axis=-1, keepdims=True)
            parts.append(part / jnp.sqrt(square + 1e-06) * gain)
        return jnp.concatenate(parts, axis=-1).astype(BF16)

    def w_wait(which, c):
        pltpu.make_async_copy(
            wqkv_ref.at[which, :, pl.ds(0, cw)], wbuf.at[which, c], w_sem.at[3 * c + which]
        ).wait()

    def keys_values(first, last):
        @pl.loop(first, last)
        def _(c):
            w_wait(1, c)
            kvbuf[0, c, 0] = rms(project(1, c), kg_ref[...])
            w_wait(2, c)
            kvbuf[0, c, 1] = project(2, c).astype(BF16)
            kv_sends(c, lambda copy: copy.start())

    def query(first, last):
        @pl.loop(first, last)
        def _(c):
            w_wait(0, c)
            qbuf[c] = rms(project(0, c), qg_ref[...])

    if pair:
        forward = [(a, 0, 0) for a in range(1, lz)]
        todo = []
        keys_values(0, chunks // 2)
        g_step(forward[0])
        keys_values(chunks // 2, chunks)
        query(0, chunks // 2)
        g_step(forward[1])
        kv_pass(0)
        query(chunks // 2, chunks)
        kv_pass(1)
        g_step(forward[2])
        for c in range(2, chunks):
            kv_pass(c)
    else:
        keys_values(0, chunks)
        for offset in offsets[1:plane]:
            g_step(offset)
        query(0, chunks)
        todo = [g for a in range(1, lz) for g in offsets[a * plane : (a + 1) * plane]]
        for c in range(chunks):
            kv_pass(c)

    factor = 1.0 / jnp.sqrt(jnp.float32(hd))
    ones = jnp.ones((1, tok), F32)
    mask = jnp.concatenate(
        [ones] + [ones * near_ref[0, j].astype(F32) for j in range(4)], axis=1
    )
    per_half = abuf.shape[3] // cw

    def attention(c):
        @pl.loop(0, 2)
        def _(k):
            at = pl.ds(pl.multiple_of(k * tok, tok), tok)
            for h in range(heads):
                cols = pl.ds(h * hd, hd)
                q = qbuf[c, at, cols]
                keys = kvbuf[:, c, 0, at, cols].reshape(5 * tok, hd)
                values = kvbuf[:, c, 1, at, cols].reshape(5 * tok, hd)
                scores = lax.dot_general(
                    q, keys, (((1,), (1,)), ((), ())), preferred_element_type=F32
                )
                expo = jnp.exp(scores * factor) * mask
                probs = (expo / jnp.sum(expo, axis=-1, keepdims=True)).astype(BF16)
                out = jnp.dot(probs, values, preferred_element_type=F32)
                abuf[c // per_half, k, :, pl.ds((c % per_half) * cw + h * hd, hd)] = out.astype(
                    BF16
                )

    def a_copy(h):
        return pltpu.make_async_remote_copy(
            src_ref=abuf.at[h],
            dst_ref=apeer.at[h],
            send_sem=a_sem.at[0, h],
            recv_sem=a_sem.at[1, h],
            device_id={"tile": t + (1 - 2 * yc) * lx},
            device_id_type=MESH,
        )

    for c in range(chunks):
        kv_rest(c)
        attention(c)
        if pair and (c + 1) % per_half == 0:
            a_copy(c // per_half).start()
        if not pair and todo:
            g_step(todo.pop(0))

    for copy in own_w:
        copy.wait()
    cached_copy.wait()
    start_copy.wait()
    flag = conv_ref[0, s] > 0

    def x_copy(k):
        return pltpu.make_async_remote_copy(
            src_ref=xsend.at[k],
            dst_ref=xrecv.at[k],
            send_sem=x_sem.at[0, k],
            recv_sem=x_sem.at[1, k],
            device_id={"step": other},
            device_id_type=MESH,
        )

    def s_copy(k):
        return pltpu.make_async_remote_copy(
            src_ref=ssend.at[k],
            dst_ref=srecv.at[k],
            send_sem=s_sem.at[0, k],
            recv_sem=s_sem.at[1, k],
            device_id={"step": other},
            device_id_type=MESH,
        )

    def y_copy(k):
        return pltpu.make_async_remote_copy(
            src_ref=ysend.at[k],
            dst_ref=yrecv.at[k],
            send_sem=y_sem.at[0, k],
            recv_sem=y_sem.at[1, k],
            device_id={"tile": t + (1 - 2 * yc) * lx},
            device_id_type=MESH,
        )

    def at_cols(b):
        block = lines[0][b // groups]
        if pair:
            block = 2 * block + (yc if b % 2 == 0 else 1 - yc)
        return pl.ds(pl.multiple_of(block * pcols, 128), pcols)

    def out_copy(b, which):
        src, dst = ((ubuf, upd_ref), (vbuf, vel_ref))[which]
        return pltpu.make_async_copy(src.at[b], dst.at[0, :, at_cols(b)], out_sem.at[which, b])

    def out_dot(k):
        which = pl.ds(lines[0][k] * plane, plane)
        for who in range(groups):
            total = None
            for h in range(2):
                weights = gbuf[h, which].reshape(pcols, hw)
                block = (abuf, apeer)[who][h].reshape(2 * tok, hw)
                term = lax.dot_general(
                    block, weights, (((1,), (1,)), ((), ())), preferred_element_type=F32
                )
                total = term if total is None else total + term
            pbuf[k, who] = total.reshape(2, tok, pcols)
            xsend[k, who] = pbuf[k, who, other].astype(BF16)
        x_copy(k).start()

    def finish(b, projected):
        velocity = jnp.where(flag, cbuf[:, at_cols(b)], gate_ref[:, at_cols(b)] * projected)
        vbuf[b] = velocity
        out_copy(b, 1).start()

        @pl.when(s == 0)
        def _():
            ssend[b] = (sizes_ref[0] * velocity).astype(BF16)
            s_copy(b).start()
            ubuf[b] = sbuf[:, at_cols(b)]
            out_copy(b, 0).start()

    def finish_own(k):
        x_copy(k).wait()
        if pair:
            ysend[k] = (pbuf[k, 1, s] + xrecv[k, 1].astype(F32)).astype(BF16)
            y_copy(k).start()
        finish(groups * k, pbuf[k, 0, s] + xrecv[k, 0].astype(F32))

    def finish_peer(k):
        if pair:
            y_copy(k).wait()
            finish(2 * k + 1, yrecv[k].astype(F32))

    def finish_later(b):
        @pl.when(s == 1)
        def _():
            s_copy(b).wait_recv()
            ubuf[b] = sbuf[:, at_cols(b)] + srecv[b].astype(F32)
            out_copy(b, 0).start()

    if pair:
        for h in range(2):
            a_copy(h).wait()
    for k in range(planes):
        if pair:
            g_step((k, 0, 1))
        else:
            while len(todo) > (planes - 1 - k) * plane:
                g_step(todo.pop(0))
        out_dot(k)
        if k >= 1:
            finish_own(k - 1)
        if k >= 2:
            finish_peer(k - 2)
            for b in range(groups * (k - 2), groups * (k - 1)):
                finish_later(b)
    finish_own(planes - 1)
    finish_peer(planes - 2)
    finish_peer(planes - 1)
    for b in range(groups * (planes - 2), groups * planes):
        finish_later(b)

    for offset in offsets:
        g_each(offset, lambda copy: copy.wait_send())

    @pl.loop(0, chunks)
    def _(c):
        kv_sends(c, lambda copy: copy.wait_send())
        if relay:
            for slot, onward, valid, peer in passed:

                @pl.when(valid)
                def _(slot=slot, onward=onward, peer=peer):
                    kv_copy(slot, onward, 0, c, peer).wait_send()

    @pl.when(s == 0)
    def _():
        for b in range(groups * planes):
            s_copy(b).wait_send()

    for b in range(groups * planes):
        out_copy(b, 0).wait()
        out_copy(b, 1).wait()


def split(tiles):
    side = int(round((tiles // 4) ** 0.5))
    assert 4 * side * side == tiles
    return (4, side, side)


def body(tiles, *args):
    (
        latents,
        start,
        cached_velocity,
        shift,
        scale,
        gate,
        step_sizes,
        converged,
        neighbours,
        w_qkv,
        q_gain,
        k_gain,
        w_out,
    ) = args
    tok, width = latents.shape[1], latents.shape[2]
    group = w_qkv.shape[2]
    hd = q_gain.shape[0]
    shard = w_out.shape[1]
    dims = split(tiles)
    planes = dims[0]
    groups = 2 if dims[1] == 2 else 1
    blocks = groups * planes
    pcols = width // blocks
    cw = 2 * hd
    chunks = group // cw
    wt = w_out.T
    any_space = pl.BlockSpec(memory_space=pl.ANY)
    vmem = pl.BlockSpec(memory_space=pltpu.VMEM)
    smem = pl.BlockSpec(memory_space=pltpu.SMEM)
    dma = pltpu.SemaphoreType.DMA
    upd, vel = pl.pallas_call(
        functools.partial(kernel, tiles, dims),
        out_shape=[jax.ShapeDtypeStruct((1, tok, width), F32)] * 2,
        in_specs=[
            vmem,
            any_space,
            any_space,
            vmem,
            vmem,
            vmem,
            smem,
            smem,
            smem,
            any_space,
            vmem,
            vmem,
            any_space,
        ],
        out_specs=[any_space, any_space],
        scratch_shapes=[
            pltpu.VMEM((2, tok, width), BF16),
            pltpu.VMEM((3, chunks, width, cw), BF16),
            pltpu.VMEM((5, chunks, 2, 2 * tok, cw), BF16),
            pltpu.VMEM((chunks, 2 * tok, cw), BF16),
            pltpu.VMEM((2, 2, tok, group // 2), BF16),
            pltpu.VMEM((2, 2, tok, group // 2), BF16),
            pltpu.VMEM((2, tiles // groups, shard, group // 2), BF16),
            pltpu.VMEM((tok, width), F32),
            pltpu.VMEM((tok, width), F32),
            pltpu.VMEM((planes, groups, 2, tok, pcols), F32),
            pltpu.VMEM((planes, groups, tok, pcols), BF16),
            pltpu.VMEM((planes, groups, tok, pcols), BF16),
            pltpu.VMEM((blocks, tok, pcols), BF16),
            pltpu.VMEM((blocks, tok, pcols), BF16),
            pltpu.VMEM((planes, tok, pcols), BF16),
            pltpu.VMEM((planes, tok, pcols), BF16),
            pltpu.VMEM((blocks, tok, pcols), F32),
            pltpu.VMEM((blocks, tok, pcols), F32),
            dma((3 * chunks,)),
            dma((4,)),
            dma((2, 2)),
            dma((5, chunks)),
            dma((5, chunks)),
            dma((2, tiles // groups, 6)),
            dma((2, tiles // groups)),
            dma((2, planes)),
            dma((2, blocks)),
            dma((2, 2)),
            dma((2, planes)),
            dma((2, blocks)),
        ],
        compiler_params=pltpu.CompilerParams(
            collective_id=0, has_side_effects=True, vmem_limit_bytes=60 * 1024 * 1024
        ),
    )(
        latents,
        start,
        cached_velocity,
        shift,
        scale,
        gate,
        step_sizes,
        converged.T,
        neighbours,
        w_qkv,
        q_gain[None],
        k_gain[None],
        wt,
    )
    return (upd, vel)


def solution(mesh):
    assert mesh.shape["step"] == 2
    placed = (
        P("step", "tile", None),
        P("tile", None),
        P("step", "tile", None),
        P("step", None),
        P("step", None),
        P("step", None),
        P("step"),
        P(None, "tile"),
        P("tile", None),
        P(None, None, "step"),
        P(),
        P(),
        P("step", "tile"),
    )
    return jax.shard_map(
        functools.partial(body, mesh.shape["tile"]),
        mesh=mesh,
        in_specs=placed,
        out_specs=(P("step", "tile", None), P("step", "tile", None)),
        check_vma=False,
    )
```

```python
import functools
import jax
import jax.numpy as jnp
from jax import lax
from jax.experimental import pallas as pl
from jax.experimental.pallas import tpu as pltpu
from jax.sharding import PartitionSpec as P

GRID_COLS = 4
MESH = pl.DeviceIdType.MESH
BF16 = jnp.bfloat16
F32 = jnp.float32


def nearest(place, length):
    if length == 1:
        return [place]
    if length == 2:
        return [place, 1 - place]
    assert length == 4
    inner = (place * (3 - place)) // 2
    flip, turn = 3 - place, lax.rem(place + 2, 4)
    beside = place + 1 - 2 * lax.rem(place, 2)
    return [
        place,
        beside,
        inner * flip + (1 - inner) * turn,
        inner * turn + (1 - inner) * flip,
    ]


def kernel(
    tiles,
    dims,
    lat_ref,
    start_ref,
    cached_ref,
    shift_ref,
    scale_ref,
    gate_ref,
    sizes_ref,
    conv_ref,
    near_ref,
    wqkv_ref,
    qg_ref,
    kg_ref,
    wt_ref,
    upd_ref,
    vel_ref,
    nbuf,
    wbuf,
    kvbuf,
    qbuf,
    abuf,
    apeer,
    gbuf,
    cbuf,
    sbuf,
    pbuf,
    xsend,
    xrecv,
    ssend,
    srecv,
    ysend,
    yrecv,
    vbuf,
    ubuf,
    w_sem,
    in_sem,
    n_sem,
    kv_send,
    kv_recv,
    g_send,
    g_recv,
    x_sem,
    s_sem,
    a_sem,
    y_sem,
    out_sem,
):
    lz, ly, lx = dims
    s = lax.axis_index("step")
    t = lax.axis_index("tile")
    other = 1 - s
    zc, yc, xc = t // (ly * lx), lax.rem(t // lx, ly), lax.rem(t, lx)
    col, row = lax.rem(t, GRID_COLS), t // GRID_COLS
    rows = tiles // GRID_COLS
    tok, width = lat_ref.shape[1], lat_ref.shape[2]
    chunks, cw = kvbuf.shape[1], kvbuf.shape[4]
    hd = qg_ref.shape[1]
    heads = cw // hd
    relay = lx == 2 and ly == 2 and GRID_COLS == 4
    pair = ly == 2
    planes = lz
    groups = 2 if pair else 1
    pcols = width // planes // groups
    plane = lx if pair else ly * lx

    strides = (ly * lx, lx, 1)
    coords = (zc, yc, xc)
    barrier = pltpu.get_barrier_semaphore()
    links = []
    for d in range(3):
        covered = strides[d] == GRID_COLS or (strides[d] == 1 and not relay)
        if dims[d] > 1 and not covered:
            links.append((coords[d] < dims[d] - 1, t + strides[d]))
            links.append((coords[d] > 0, t - strides[d]))
    if not relay:
        links.append((col < GRID_COLS - 1, t + 1))
        links.append((col > 0, t - 1))
    links.append((row < rows - 1, t + GRID_COLS))
    links.append((row > 0, t - GRID_COLS))
    pl.semaphore_signal(barrier, inc=1, device_id={"step": other}, device_id_type=MESH)
    for valid, peer in links:

        @pl.when(valid)
        def _(peer=peer):
            pl.semaphore_signal(barrier, inc=1, device_id={"tile": peer}, device_id_type=MESH)

    def w_copy(i):
        return pltpu.make_async_copy(
            wqkv_ref.at[i % 3, :, pl.ds((i // 3) * cw, cw)], wbuf.at[i % 3, i // 3], w_sem.at[i]
        )

    for c in range(chunks):
        w_copy(3 * c + 1).start()
        w_copy(3 * c + 2).start()
    for c in range(chunks):
        w_copy(3 * c).start()
    hw = gbuf.shape[3]

    def spot(tile):
        return (tile // (ly * lx)) * lx + lax.rem(tile, lx) if pair else tile

    own_w = [
        pltpu.make_async_copy(wt_ref.at[:, pl.ds(h * hw, hw)], gbuf.at[h, spot(t)], in_sem.at[h])
        for h in range(2)
    ]
    for copy in own_w:
        copy.start()
    cached_copy = pltpu.make_async_copy(cached_ref.at[0], cbuf, in_sem.at[2])
    start_copy = pltpu.make_async_copy(start_ref, sbuf, in_sem.at[3])
    cached_copy.start()
    start_copy.start()

    pl.semaphore_wait(barrier, 1 + sum(valid.astype(jnp.int32) for valid, _ in links))

    orders = ((0, 2), (0, 2)) if pair else ((0, 1, 2), (0, 2, 1))
    lines = [nearest(coords[d], dims[d]) for d in range(3)]

    def g_copy(h, source, src, d, up):
        peer = t + strides[d] if up else t - strides[d]
        return pltpu.make_async_remote_copy(
            src_ref=src,
            dst_ref=gbuf.at[h, spot(source)],
            send_sem=g_send.at[h, spot(source), 2 * d + (1 if up else 0)],
            recv_sem=g_recv.at[h, spot(source)],
            device_id={"tile": peer},
            device_id_type=MESH,
        )

    def g_each(offset, act):
        source = sum(lines[d][offset[d]] * strides[d] for d in range(3))
        for h in range(2):
            order = orders[h]
            for j in range(len(order)):
                d = order[j]
                if any(offset[e] != 0 for e in order[j + 1 :]):
                    continue
                for up in (True, False):
                    if up:
                        valid = coords[d] < dims[d] - 1
                    else:
                        valid = coords[d] > 0
                    if offset[d] != 0:
                        if dims[d] == 2:
                            continue
                        place = lines[d][offset[d]]
                        away = coords[d] > place if up else coords[d] < place
                        valid = jnp.logical_and(valid, away)

                    @pl.when(valid)
                    def _(h=h, d=d, up=up):
                        own = offset == (0, 0, 0)
                        src = wt_ref.at[:, pl.ds(h * hw, hw)] if own else gbuf.at[h, spot(source)]
                        act(g_copy(h, source, src, d, up))

    def g_step(offset):
        if offset != (0, 0, 0):
            source = sum(lines[d][offset[d]] * strides[d] for d in range(3))
            for h in range(2):
                pltpu.make_async_remote_copy(
                    src_ref=gbuf.at[h, spot(source)],
                    dst_ref=gbuf.at[h, spot(source)],
                    send_sem=g_send.at[h, spot(source), 0],
                    recv_sem=g_recv.at[h, spot(source)],
                    device_id={"step": other},
                    device_id_type=MESH,
                ).wait_recv()
        g_each(offset, lambda copy: copy.start())

    offsets = [
        (a, b, c)
        for a in range(dims[0])
        for b, c in sorted(
            [(b, c) for b in range(1 if pair else dims[1]) for c in range(dims[2])], key=lambda v: v[0] + v[1]
        )
    ]
    g_step((0, 0, 0))

    def n_copy(part):
        half = tok // 2
        where = nbuf.at[s, pl.ds(part * half, half)]
        return pltpu.make_async_remote_copy(
            src_ref=where,
            dst_ref=where,
            send_sem=n_sem.at[0, part],
            recv_sem=n_sem.at[1, part],
            device_id={"step": other},
            device_id_type=MESH,
        )

    for part in range(2):
        half = tok // 2
        own = lat_ref[0, pl.ds(part * half, half), :]
        mean = jnp.mean(own, axis=-1, keepdims=True)
        cent = own - mean
        var = jnp.mean(cent * cent, axis=-1, keepdims=True)
        normed = cent * (1.0 / jnp.sqrt(var + 1e-06)) * (1.0 + scale_ref[...]) + shift_ref[...]
        nbuf[s, pl.ds(part * half, half), :] = normed.astype(BF16)
        n_copy(part).start()

    present = (None, col > 0, col < GRID_COLS - 1, row > 0, row < rows - 1)
    for j in range(1, 5):

        @pl.when(jnp.logical_not(present[j]))
        def _(j=j):
            @pl.loop(0, chunks)
            def _(c):
                kvbuf[j, c] = jnp.zeros(kvbuf.shape[2:], BF16)

    for part in range(2):
        n_copy(part).wait()

    def kv_copy(src_slot, slot, sem, c, peer):
        return pltpu.make_async_remote_copy(
            src_ref=kvbuf.at[src_slot, c],
            dst_ref=kvbuf.at[slot, c],
            send_sem=kv_send.at[sem, c],
            recv_sem=kv_recv.at[slot, c],
            device_id={"tile": peer},
            device_id_type=MESH,
        )

    right, left = col < GRID_COLS - 1, col > 0
    if relay:
        right, left = lax.rem(col, 2) == 0, lax.rem(col, 2) == 1
    sends = (
        (1, right, t + 1),
        (2, left, t - 1),
        (3, row < rows - 1, t + GRID_COLS),
        (4, row > 0, t - GRID_COLS),
    )

    def kv_sends(c, act):
        for slot, valid, peer in sends:

            @pl.when(valid)
            def _(slot=slot, peer=peer):
                act(kv_copy(0, slot, slot, c, peer))

    passed = ((2, 1, col == 0, t + 2), (1, 2, col == 3, t - 2))

    def kv_wait(c, slots):
        for slot in slots:

            @pl.when(present[slot])
            def _(slot=slot):
                pltpu.make_async_remote_copy(
                    src_ref=kvbuf.at[slot, c],
                    dst_ref=kvbuf.at[slot, c],
                    send_sem=kv_send.at[slot, c],
                    recv_sem=kv_recv.at[slot, c],
                    device_id={"step": other},
                    device_id_type=MESH,
                ).wait_recv()

    def kv_pass(c):
        if not relay:
            return
        for slot, onward, valid, peer in passed:

            @pl.when(lax.rem(col, 2) == (0 if slot == 2 else 1))
            def _(slot=slot):
                pltpu.make_async_remote_copy(
                    src_ref=kvbuf.at[slot, c],
                    dst_ref=kvbuf.at[slot, c],
                    send_sem=kv_send.at[slot, c],
                    recv_sem=kv_recv.at[slot, c],
                    device_id={"step": other},
                    device_id_type=MESH,
                ).wait_recv()

            @pl.when(valid)
            def _(slot=slot, onward=onward, peer=peer):
                kv_copy(slot, onward, 0, c, peer).start()

    def kv_rest(c):
        if not relay:
            kv_wait(c, (1, 2, 3, 4))
            return
        for slot, valid in ((1, col == 2), (2, col == 1)):

            @pl.when(valid)
            def _(slot=slot):
                pltpu.make_async_remote_copy(
                    src_ref=kvbuf.at[slot, c],
                    dst_ref=kvbuf.at[slot, c],
                    send_sem=kv_send.at[slot, c],
                    recv_sem=kv_recv.at[slot, c],
                    device_id={"step": other},
                    device_id_type=MESH,
                ).wait_recv()

        kv_wait(c, (3, 4))

    def project(which, c):
        block = nbuf[...].reshape(2 * tok, width)
        return jnp.dot(block, wbuf[which, c], preferred_element_type=F32)

    def rms(result, gain):
        parts = []
        for h in range(heads):
            part = result[:, h * hd : (h + 1) * hd]
            square = jnp.mean(part * part, axis=-1, keepdims=True)
            parts.append(part * (1.0 / jnp.sqrt(square + 1e-06)) * gain)
        return jnp.concatenate(parts, axis=-1).astype(BF16)

    def w_wait(which, c):
        pltpu.make_async_copy(
            wqkv_ref.at[which, :, pl.ds(0, cw)], wbuf.at[which, c], w_sem.at[3 * c + which]
        ).wait()

    def keys_values(first, last):
        @pl.loop(first, last)
        def _(c):
            w_wait(1, c)
            kvbuf[0, c, 0] = rms(project(1, c), kg_ref[...])
            w_wait(2, c)
            kvbuf[0, c, 1] = project(2, c).astype(BF16)
            kv_sends(c, lambda copy: copy.start())

    def query(first, last):
        @pl.loop(first, last)
        def _(c):
            w_wait(0, c)
            qbuf[c] = rms(project(0, c), qg_ref[...])

    if pair:
        forward = [(a, 0, 0) for a in range(1, lz)]
        todo = []
        keys_values(0, chunks)
        query(0, chunks // 2)
        g_step(forward[0])
        kv_pass(0)
        query(chunks // 2, chunks)
        kv_pass(1)
        g_step(forward[1])
        for c in range(2, chunks):
            kv_pass(c)
        g_step(forward[2])
    else:
        keys_values(0, chunks)
        for offset in offsets[1:plane]:
            g_step(offset)
        query(0, chunks)
        todo = [g for a in range(1, lz) for g in offsets[a * plane : (a + 1) * plane]]
        for c in range(chunks):
            kv_pass(c)

    factor = 1.0 / jnp.sqrt(jnp.float32(hd))
    ones = jnp.ones((1, tok), F32)
    mask = jnp.concatenate(
        [ones] + [ones * near_ref[0, j].astype(F32) for j in range(4)], axis=1
    )
    per_half = abuf.shape[3] // cw

    def attention(c):
        for k in range(2):
            at = pl.ds(k * tok, tok)
            for h in range(heads):
                cols = pl.ds(h * hd, hd)
                q = qbuf[c, at, cols]
                keys = kvbuf[:, c, 0, at, cols].reshape(5 * tok, hd)
                values = kvbuf[:, c, 1, at, cols].reshape(5 * tok, hd)
                scores = lax.dot_general(
                    q, keys, (((1,), (1,)), ((), ())), preferred_element_type=F32
                )
                expo = jnp.exp(scores * factor) * mask
                probs = (expo * (1.0 / jnp.sum(expo, axis=-1, keepdims=True))).astype(BF16)
                out = jnp.dot(probs, values, preferred_element_type=F32)
                abuf[c // per_half, k, :, pl.ds((c % per_half) * cw + h * hd, hd)] = out.astype(
                    BF16
                )

    def a_copy(h):
        return pltpu.make_async_remote_copy(
            src_ref=abuf.at[h],
            dst_ref=apeer.at[h],
            send_sem=a_sem.at[0, h],
            recv_sem=a_sem.at[1, h],
            device_id={"tile": t + (1 - 2 * yc) * lx},
            device_id_type=MESH,
        )

    for c in range(chunks):
        kv_rest(c)
        attention(c)
        if pair and (c + 1) % per_half == 0:
            a_copy(c // per_half).start()
        if not pair and todo:
            g_step(todo.pop(0))

    for copy in own_w:
        copy.wait()
    cached_copy.wait()
    start_copy.wait()
    flag = conv_ref[0, s] > 0

    def x_copy(k):
        return pltpu.make_async_remote_copy(
            src_ref=xsend.at[k],
            dst_ref=xrecv.at[k],
            send_sem=x_sem.at[0, k],
            recv_sem=x_sem.at[1, k],
            device_id={"step": other},
            device_id_type=MESH,
        )

    def s_copy(k):
        return pltpu.make_async_remote_copy(
            src_ref=ssend.at[k],
            dst_ref=srecv.at[k],
            send_sem=s_sem.at[0, k],
            recv_sem=s_sem.at[1, k],
            device_id={"step": other},
            device_id_type=MESH,
        )

    def y_copy(k):
        return pltpu.make_async_remote_copy(
            src_ref=ysend.at[k],
            dst_ref=yrecv.at[k],
            send_sem=y_sem.at[0, k],
            recv_sem=y_sem.at[1, k],
            device_id={"tile": t + (1 - 2 * yc) * lx},
            device_id_type=MESH,
        )

    def at_cols(b):
        block = lines[0][b // groups]
        if pair:
            block = 2 * block + (yc if b % 2 == 0 else 1 - yc)
        return pl.ds(pl.multiple_of(block * pcols, 128), pcols)

    def out_copy(b, which):
        src, dst = ((ubuf, upd_ref), (vbuf, vel_ref))[which]
        return pltpu.make_async_copy(src.at[b], dst.at[0, :, at_cols(b)], out_sem.at[which, b])

    def out_dot(k):
        which = pl.ds(lines[0][k] * plane, plane)
        for who in range(groups):
            total = None
            for h in range(2):
                weights = gbuf[h, which].reshape(pcols, hw)
                block = (abuf, apeer)[who][h].reshape(2 * tok, hw)
                term = lax.dot_general(
                    block, weights, (((1,), (1,)), ((), ())), preferred_element_type=F32
                )
                total = term if total is None else total + term
            pbuf[k, who] = total.reshape(2, tok, pcols)
            xsend[k, who] = pbuf[k, who, other].astype(BF16)
        x_copy(k).start()

    def finish(b, projected):
        velocity = jnp.where(flag, cbuf[:, at_cols(b)], gate_ref[:, at_cols(b)] * projected)
        vbuf[b] = velocity
        out_copy(b, 1).start()

        @pl.when(s == 0)
        def _():
            ssend[b] = (sizes_ref[0] * velocity).astype(BF16)
            s_copy(b).start()
            ubuf[b] = sbuf[:, at_cols(b)]
            out_copy(b, 0).start()

    def finish_own(k):
        x_copy(k).wait()
        if pair:
            ysend[k] = (pbuf[k, 1, s] + xrecv[k, 1].astype(F32)).astype(BF16)
            y_copy(k).start()
        finish(groups * k, pbuf[k, 0, s] + xrecv[k, 0].astype(F32))

    def finish_peer(k):
        if pair:
            y_copy(k).wait()
            finish(2 * k + 1, yrecv[k].astype(F32))

    def finish_later(b):
        @pl.when(s == 1)
        def _():
            s_copy(b).wait_recv()
            ubuf[b] = sbuf[:, at_cols(b)] + srecv[b].astype(F32)
            out_copy(b, 0).start()

    if pair:
        for h in range(2):
            a_copy(h).wait()
    for k in range(planes):
        if pair:
            g_step((k, 0, 1))
        else:
            while len(todo) > (planes - 1 - k) * plane:
                g_step(todo.pop(0))
        out_dot(k)
        if k >= 1:
            finish_own(k - 1)
        if k >= 2:
            finish_peer(k - 2)
            for b in range(groups * (k - 2), groups * (k - 1)):
                finish_later(b)
    finish_own(planes - 1)
    finish_peer(planes - 2)
    finish_peer(planes - 1)
    for b in range(groups * (planes - 2), groups * planes):
        finish_later(b)

    for offset in offsets:
        g_each(offset, lambda copy: copy.wait_send())

    @pl.loop(0, chunks)
    def _(c):
        kv_sends(c, lambda copy: copy.wait_send())
        if relay:
            for slot, onward, valid, peer in passed:

                @pl.when(valid)
                def _(slot=slot, onward=onward, peer=peer):
                    kv_copy(slot, onward, 0, c, peer).wait_send()

    @pl.when(s == 0)
    def _():
        for b in range(groups * planes):
            s_copy(b).wait_send()

    for b in range(groups * planes):
        out_copy(b, 0).wait()
        out_copy(b, 1).wait()


def split(tiles):
    side = int(round((tiles // 4) ** 0.5))
    assert 4 * side * side == tiles
    return (4, side, side)


def body(tiles, *args):
    (
        latents,
        start,
        cached_velocity,
        shift,
        scale,
        gate,
        step_sizes,
        converged,
        neighbours,
        w_qkv,
        q_gain,
        k_gain,
        w_out,
    ) = args
    tok, width = latents.shape[1], latents.shape[2]
    group = w_qkv.shape[2]
    hd = q_gain.shape[0]
    shard = w_out.shape[1]
    dims = split(tiles)
    planes = dims[0]
    groups = 2 if dims[1] == 2 else 1
    blocks = groups * planes
    pcols = width // blocks
    cw = 2 * hd
    chunks = group // cw
    wt = w_out.T
    any_space = pl.BlockSpec(memory_space=pl.ANY)
    vmem = pl.BlockSpec(memory_space=pltpu.VMEM)
    smem = pl.BlockSpec(memory_space=pltpu.SMEM)
    dma = pltpu.SemaphoreType.DMA
    upd, vel = pl.pallas_call(
        functools.partial(kernel, tiles, dims),
        out_shape=[jax.ShapeDtypeStruct((1, tok, width), F32)] * 2,
        in_specs=[
            vmem,
            any_space,
            any_space,
            vmem,
            vmem,
            vmem,
            smem,
            smem,
            smem,
            any_space,
            vmem,
            vmem,
            any_space,
        ],
        out_specs=[any_space, any_space],
        scratch_shapes=[
            pltpu.VMEM((2, tok, width), BF16),
            pltpu.VMEM((3, chunks, width, cw), BF16),
            pltpu.VMEM((5, chunks, 2, 2 * tok, cw), BF16),
            pltpu.VMEM((chunks, 2 * tok, cw), BF16),
            pltpu.VMEM((2, 2, tok, group // 2), BF16),
            pltpu.VMEM((2, 2, tok, group // 2), BF16),
            pltpu.VMEM((2, tiles // groups, shard, group // 2), BF16),
            pltpu.VMEM((tok, width), F32),
            pltpu.VMEM((tok, width), F32),
            pltpu.VMEM((planes, groups, 2, tok, pcols), F32),
            pltpu.VMEM((planes, groups, tok, pcols), BF16),
            pltpu.VMEM((planes, groups, tok, pcols), BF16),
            pltpu.VMEM((blocks, tok, pcols), BF16),
            pltpu.VMEM((blocks, tok, pcols), BF16),
            pltpu.VMEM((planes, tok, pcols), BF16),
            pltpu.VMEM((planes, tok, pcols), BF16),
            pltpu.VMEM((blocks, tok, pcols), F32),
            pltpu.VMEM((blocks, tok, pcols), F32),
            dma((3 * chunks,)),
            dma((4,)),
            dma((2, 2)),
            dma((5, chunks)),
            dma((5, chunks)),
            dma((2, tiles // groups, 6)),
            dma((2, tiles // groups)),
            dma((2, planes)),
            dma((2, blocks)),
            dma((2, 2)),
            dma((2, planes)),
            dma((2, blocks)),
        ],
        compiler_params=pltpu.CompilerParams(
            collective_id=0, has_side_effects=True, vmem_limit_bytes=60 * 1024 * 1024
        ),
    )(
        latents,
        start,
        cached_velocity,
        shift,
        scale,
        gate,
        step_sizes,
        converged.T,
        neighbours,
        w_qkv,
        q_gain[None],
        k_gain[None],
        wt,
    )
    return (upd, vel)


def solution(mesh):
    assert mesh.shape["step"] == 2
    placed = (
        P("step", "tile", None),
        P("tile", None),
        P("step", "tile", None),
        P("step", None),
        P("step", None),
        P("step", None),
        P("step"),
        P(None, "tile"),
        P("tile", None),
        P(None, None, "step"),
        P(),
        P(),
        P("step", "tile"),
    )
    return jax.shard_map(
        functools.partial(body, mesh.shape["tile"]),
        mesh=mesh,
        in_specs=placed,
        out_specs=(P("step", "tile", None), P("step", "tile", None)),
        check_vma=False,
    )
```

```python
import functools
import jax
import jax.numpy as jnp
from jax import lax
from jax.experimental import pallas as pl
from jax.experimental.pallas import tpu as pltpu
from jax.sharding import PartitionSpec as P

GRID_COLS = 4
MESH = pl.DeviceIdType.MESH
BF16 = jnp.bfloat16
F32 = jnp.float32


def nearest(place, length):
    if length == 1:
        return [place]
    if length == 2:
        return [place, 1 - place]
    assert length == 4
    inner = (place * (3 - place)) // 2
    flip, turn = 3 - place, lax.rem(place + 2, 4)
    beside = place + 1 - 2 * lax.rem(place, 2)
    return [
        place,
        beside,
        inner * flip + (1 - inner) * turn,
        inner * turn + (1 - inner) * flip,
    ]


def kernel(
    tiles,
    dims,
    lat_ref,
    start_ref,
    cached_ref,
    shift_ref,
    scale_ref,
    gate_ref,
    sizes_ref,
    conv_ref,
    near_ref,
    wqkv_ref,
    qg_ref,
    kg_ref,
    wt_ref,
    upd_ref,
    vel_ref,
    nbuf,
    wbuf,
    kvbuf,
    qbuf,
    abuf,
    apeer,
    gbuf,
    cbuf,
    sbuf,
    pbuf,
    xsend,
    xrecv,
    ssend,
    srecv,
    ysend,
    yrecv,
    vbuf,
    ubuf,
    w_sem,
    in_sem,
    n_sem,
    kv_send,
    kv_recv,
    g_send,
    g_recv,
    x_sem,
    s_sem,
    a_sem,
    y_sem,
    out_sem,
):
    lz, ly, lx = dims
    s = lax.axis_index("step")
    t = lax.axis_index("tile")
    other = 1 - s
    zc, yc, xc = t // (ly * lx), lax.rem(t // lx, ly), lax.rem(t, lx)
    col, row = lax.rem(t, GRID_COLS), t // GRID_COLS
    rows = tiles // GRID_COLS
    tok, width = lat_ref.shape[1], lat_ref.shape[2]
    chunks, cw = kvbuf.shape[1], kvbuf.shape[4]
    hd = qg_ref.shape[1]
    heads = cw // hd
    relay = lx == 2 and ly == 2 and GRID_COLS == 4
    pair = ly == 2
    planes = lz
    groups = 2 if pair else 1
    pcols = width // planes // groups
    plane = lx if pair else ly * lx

    strides = (ly * lx, lx, 1)
    coords = (zc, yc, xc)
    barrier = pltpu.get_barrier_semaphore()
    links = []
    for d in range(3):
        covered = strides[d] == GRID_COLS or (strides[d] == 1 and not relay)
        if dims[d] > 1 and not covered:
            links.append((coords[d] < dims[d] - 1, t + strides[d]))
            links.append((coords[d] > 0, t - strides[d]))
    if not relay:
        links.append((col < GRID_COLS - 1, t + 1))
        links.append((col > 0, t - 1))
    links.append((row < rows - 1, t + GRID_COLS))
    links.append((row > 0, t - GRID_COLS))
    pl.semaphore_signal(barrier, inc=1, device_id={"step": other}, device_id_type=MESH)
    for valid, peer in links:

        @pl.when(valid)
        def _(peer=peer):
            pl.semaphore_signal(barrier, inc=1, device_id={"tile": peer}, device_id_type=MESH)

    def w_copy(i):
        return pltpu.make_async_copy(
            wqkv_ref.at[i % 3, :, pl.ds((i // 3) * cw, cw)], wbuf.at[i % 3, i // 3], w_sem.at[i]
        )

    for c in range(chunks):
        w_copy(3 * c + 1).start()
        w_copy(3 * c + 2).start()
    for c in range(chunks):
        w_copy(3 * c).start()
    hw = gbuf.shape[3]

    def spot(tile):
        return (tile // (ly * lx)) * lx + lax.rem(tile, lx) if pair else tile

    own_w = [
        pltpu.make_async_copy(wt_ref.at[:, pl.ds(h * hw, hw)], gbuf.at[h, spot(t)], in_sem.at[h])
        for h in range(2)
    ]
    for copy in own_w:
        copy.start()
    cached_copy = pltpu.make_async_copy(cached_ref.at[0], cbuf, in_sem.at[2])
    start_copy = pltpu.make_async_copy(start_ref, sbuf, in_sem.at[3])
    cached_copy.start()
    start_copy.start()

    pl.semaphore_wait(barrier, 1 + sum(valid.astype(jnp.int32) for valid, _ in links))

    orders = ((0, 2), (0, 2)) if pair else ((0, 1, 2), (0, 2, 1))
    lines = [nearest(coords[d], dims[d]) for d in range(3)]

    def g_copy(h, source, src, d, up):
        peer = t + strides[d] if up else t - strides[d]
        return pltpu.make_async_remote_copy(
            src_ref=src,
            dst_ref=gbuf.at[h, spot(source)],
            send_sem=g_send.at[h, spot(source), 2 * d + (1 if up else 0)],
            recv_sem=g_recv.at[h, spot(source)],
            device_id={"tile": peer},
            device_id_type=MESH,
        )

    def g_each(offset, act):
        source = sum(lines[d][offset[d]] * strides[d] for d in range(3))
        for h in range(2):
            order = orders[h]
            for j in range(len(order)):
                d = order[j]
                if any(offset[e] != 0 for e in order[j + 1 :]):
                    continue
                for up in (True, False):
                    if up:
                        valid = coords[d] < dims[d] - 1
                    else:
                        valid = coords[d] > 0
                    if offset[d] != 0:
                        if dims[d] == 2:
                            continue
                        place = lines[d][offset[d]]
                        away = coords[d] > place if up else coords[d] < place
                        valid = jnp.logical_and(valid, away)

                    @pl.when(valid)
                    def _(h=h, d=d, up=up):
                        own = offset == (0, 0, 0)
                        src = wt_ref.at[:, pl.ds(h * hw, hw)] if own else gbuf.at[h, spot(source)]
                        act(g_copy(h, source, src, d, up))

    def g_step(offset):
        if offset != (0, 0, 0):
            source = sum(lines[d][offset[d]] * strides[d] for d in range(3))
            for h in range(2):
                pltpu.make_async_remote_copy(
                    src_ref=gbuf.at[h, spot(source)],
                    dst_ref=gbuf.at[h, spot(source)],
                    send_sem=g_send.at[h, spot(source), 0],
                    recv_sem=g_recv.at[h, spot(source)],
                    device_id={"step": other},
                    device_id_type=MESH,
                ).wait_recv()
        g_each(offset, lambda copy: copy.start())

    offsets = [
        (a, b, c)
        for a in range(dims[0])
        for b, c in sorted(
            [(b, c) for b in range(1 if pair else dims[1]) for c in range(dims[2])], key=lambda v: v[0] + v[1]
        )
    ]
    g_step((0, 0, 0))

    def n_copy(part):
        half = tok // 2
        where = nbuf.at[s, pl.ds(part * half, half)]
        return pltpu.make_async_remote_copy(
            src_ref=where,
            dst_ref=where,
            send_sem=n_sem.at[0, part],
            recv_sem=n_sem.at[1, part],
            device_id={"step": other},
            device_id_type=MESH,
        )

    for part in range(2):
        half = tok // 2
        own = lat_ref[0, pl.ds(part * half, half), :]
        mean = jnp.mean(own, axis=-1, keepdims=True)
        cent = own - mean
        var = jnp.mean(cent * cent, axis=-1, keepdims=True)
        normed = cent * (1.0 / jnp.sqrt(var + 1e-06)) * (1.0 + scale_ref[...]) + shift_ref[...]
        nbuf[s, pl.ds(part * half, half), :] = normed.astype(BF16)
        n_copy(part).start()

    present = (None, col > 0, col < GRID_COLS - 1, row > 0, row < rows - 1)
    for j in range(1, 5):

        @pl.when(jnp.logical_not(present[j]))
        def _(j=j):
            @pl.loop(0, chunks)
            def _(c):
                kvbuf[j, c] = jnp.zeros(kvbuf.shape[2:], BF16)

    for part in range(2):
        n_copy(part).wait()

    def kv_copy(src_slot, slot, sem, c, peer):
        return pltpu.make_async_remote_copy(
            src_ref=kvbuf.at[src_slot, c],
            dst_ref=kvbuf.at[slot, c],
            send_sem=kv_send.at[sem, c],
            recv_sem=kv_recv.at[slot, c],
            device_id={"tile": peer},
            device_id_type=MESH,
        )

    right, left = col < GRID_COLS - 1, col > 0
    if relay:
        right, left = lax.rem(col, 2) == 0, lax.rem(col, 2) == 1
    sends = (
        (1, right, t + 1),
        (2, left, t - 1),
        (3, row < rows - 1, t + GRID_COLS),
        (4, row > 0, t - GRID_COLS),
    )

    def kv_sends(c, act):
        for slot, valid, peer in sends:

            @pl.when(valid)
            def _(slot=slot, peer=peer):
                act(kv_copy(0, slot, slot, c, peer))

    passed = ((2, 1, col == 0, t + 2), (1, 2, col == 3, t - 2))

    def kv_wait(c, slots):
        for slot in slots:

            @pl.when(present[slot])
            def _(slot=slot):
                pltpu.make_async_remote_copy(
                    src_ref=kvbuf.at[slot, c],
                    dst_ref=kvbuf.at[slot, c],
                    send_sem=kv_send.at[slot, c],
                    recv_sem=kv_recv.at[slot, c],
                    device_id={"step": other},
                    device_id_type=MESH,
                ).wait_recv()

    def kv_pass(c):
        if not relay:
            return
        for slot, onward, valid, peer in passed:

            @pl.when(lax.rem(col, 2) == (0 if slot == 2 else 1))
            def _(slot=slot):
                pltpu.make_async_remote_copy(
                    src_ref=kvbuf.at[slot, c],
                    dst_ref=kvbuf.at[slot, c],
                    send_sem=kv_send.at[slot, c],
                    recv_sem=kv_recv.at[slot, c],
                    device_id={"step": other},
                    device_id_type=MESH,
                ).wait_recv()

            @pl.when(valid)
            def _(slot=slot, onward=onward, peer=peer):
                kv_copy(slot, onward, 0, c, peer).start()

    def kv_rest(c):
        if not relay:
            kv_wait(c, (1, 2, 3, 4))
            return
        for slot, valid in ((1, col == 2), (2, col == 1)):

            @pl.when(valid)
            def _(slot=slot):
                pltpu.make_async_remote_copy(
                    src_ref=kvbuf.at[slot, c],
                    dst_ref=kvbuf.at[slot, c],
                    send_sem=kv_send.at[slot, c],
                    recv_sem=kv_recv.at[slot, c],
                    device_id={"step": other},
                    device_id_type=MESH,
                ).wait_recv()

        kv_wait(c, (3, 4))

    def project(which, c):
        block = nbuf[...].reshape(2 * tok, width)
        return jnp.dot(block, wbuf[which, c], preferred_element_type=F32)

    def rms(result, gain):
        parts = []
        for h in range(heads):
            part = result[:, h * hd : (h + 1) * hd]
            square = jnp.mean(part * part, axis=-1, keepdims=True)
            parts.append(part * (1.0 / jnp.sqrt(square + 1e-06)) * gain)
        return jnp.concatenate(parts, axis=-1).astype(BF16)

    def w_wait(which, c):
        pltpu.make_async_copy(
            wqkv_ref.at[which, :, pl.ds(0, cw)], wbuf.at[which, c], w_sem.at[3 * c + which]
        ).wait()

    def keys_values(first, last):
        @pl.loop(first, last)
        def _(c):
            w_wait(1, c)
            kvbuf[0, c, 0] = rms(project(1, c), kg_ref[...])
            w_wait(2, c)
            kvbuf[0, c, 1] = project(2, c).astype(BF16)
            kv_sends(c, lambda copy: copy.start())

    def query(first, last):
        @pl.loop(first, last)
        def _(c):
            w_wait(0, c)
            qbuf[c] = rms(project(0, c), qg_ref[...])

    if pair:
        forward = [(a, 0, 0) for a in range(1, lz)]
        todo = []
        keys_values(0, chunks)
        query(0, chunks // 2)
        g_step(forward[0])
        kv_pass(0)
        query(chunks // 2, chunks)
        kv_pass(1)
        g_step(forward[1])
        for c in range(2, chunks):
            kv_pass(c)
        g_step(forward[2])
    else:
        keys_values(0, chunks)
        for offset in offsets[1:plane]:
            g_step(offset)
        query(0, chunks)
        todo = [g for a in range(1, lz) for g in offsets[a * plane : (a + 1) * plane]]
        for c in range(chunks):
            kv_pass(c)

    factor = 1.0 / jnp.sqrt(jnp.float32(hd))
    ones = jnp.ones((1, tok), F32)
    mask = jnp.concatenate(
        [ones] + [ones * near_ref[0, j].astype(F32) for j in range(4)], axis=1
    )

    def attention(c):
        for k in range(2):
            at = pl.ds(k * tok, tok)
            for h in range(heads):
                cols = pl.ds(h * hd, hd)
                q = qbuf[c, at, cols]
                keys = kvbuf[:, c, 0, at, cols].reshape(5 * tok, hd)
                values = kvbuf[:, c, 1, at, cols].reshape(5 * tok, hd)
                scores = lax.dot_general(
                    q, keys, (((1,), (1,)), ((), ())), preferred_element_type=F32
                )
                expo = jnp.exp(scores * factor) * mask
                probs = (expo * (1.0 / jnp.sum(expo, axis=-1, keepdims=True))).astype(BF16)
                out = jnp.dot(probs, values, preferred_element_type=F32)
                abuf[c, k, :, pl.ds(h * hd, hd)] = out.astype(BF16)

    def a_copy(h):
        return pltpu.make_async_remote_copy(
            src_ref=abuf.at[h],
            dst_ref=apeer.at[h],
            send_sem=a_sem.at[0, h],
            recv_sem=a_sem.at[1, h],
            device_id={"tile": t + (1 - 2 * yc) * lx},
            device_id_type=MESH,
        )

    for c in range(chunks):
        kv_rest(c)
        attention(c)
        if pair:
            a_copy(c).start()
        if not pair and todo:
            g_step(todo.pop(0))

    for copy in own_w:
        copy.wait()
    cached_copy.wait()
    start_copy.wait()
    flag = conv_ref[0, s] > 0

    def x_copy(b):
        return pltpu.make_async_remote_copy(
            src_ref=xsend.at[b // groups, b % groups],
            dst_ref=xrecv.at[b // groups, b % groups],
            send_sem=x_sem.at[0, b],
            recv_sem=x_sem.at[1, b],
            device_id={"step": other},
            device_id_type=MESH,
        )

    def s_copy(k):
        return pltpu.make_async_remote_copy(
            src_ref=ssend.at[k],
            dst_ref=srecv.at[k],
            send_sem=s_sem.at[0, k],
            recv_sem=s_sem.at[1, k],
            device_id={"step": other},
            device_id_type=MESH,
        )

    def y_copy(k):
        return pltpu.make_async_remote_copy(
            src_ref=ysend.at[k],
            dst_ref=yrecv.at[k],
            send_sem=y_sem.at[0, k],
            recv_sem=y_sem.at[1, k],
            device_id={"tile": t + (1 - 2 * yc) * lx},
            device_id_type=MESH,
        )

    def at_cols(b):
        block = lines[0][b // groups]
        if pair:
            block = 2 * block + (yc if b % 2 == 0 else 1 - yc)
        return pl.ds(pl.multiple_of(block * pcols, 128), pcols)

    def out_copy(b, which):
        src, dst = ((ubuf, upd_ref), (vbuf, vel_ref))[which]
        return pltpu.make_async_copy(src.at[b], dst.at[0, :, at_cols(b)], out_sem.at[which, b])

    def out_dot(b):
        k, who = b // groups, b % groups
        which = pl.ds(lines[0][k] * plane, plane)
        total = None
        per_half = hw // cw
        for h in range(2):
            weights = gbuf[h, which].reshape(pcols, hw)
            for i in range(per_half):
                block = (abuf, apeer)[who][h * per_half + i].reshape(2 * tok, cw)
                term = lax.dot_general(
                    block,
                    weights[:, i * cw : (i + 1) * cw],
                    (((1,), (1,)), ((), ())),
                    preferred_element_type=F32,
                )
                total = term if total is None else total + term
        pbuf[k, who] = total.reshape(2, tok, pcols)
        xsend[k, who] = pbuf[k, who, other].astype(BF16)
        x_copy(b).start()

    def finish(b, projected):
        velocity = jnp.where(flag, cbuf[:, at_cols(b)], gate_ref[:, at_cols(b)] * projected)
        vbuf[b] = velocity
        out_copy(b, 1).start()

        @pl.when(s == 0)
        def _():
            ssend[b] = (sizes_ref[0] * velocity).astype(BF16)
            s_copy(b).start()
            ubuf[b] = sbuf[:, at_cols(b)]
            out_copy(b, 0).start()

    def reduce(b):
        k, who = b // groups, b % groups
        x_copy(b).wait()
        projected = pbuf[k, who, s] + xrecv[k, who].astype(F32)
        if who == 1:
            ysend[k] = projected.astype(BF16)
            y_copy(k).start()
        else:
            finish(b, projected)

    def finish_peer(b):
        if b % groups == 1:
            y_copy(b // groups).wait()
            finish(b, yrecv[b // groups].astype(F32))

    def finish_later(b):
        @pl.when(s == 1)
        def _():
            s_copy(b).wait_recv()
            ubuf[b] = sbuf[:, at_cols(b)] + srecv[b].astype(F32)
            out_copy(b, 0).start()

    if pair:
        items = [0, 1]
        for k in range(1, planes):
            items += [2 * k + 1, 2 * k]
    else:
        items = list(range(planes))
    ready = set()
    steps = (reduce, finish_peer, finish_later)
    lags = (1, 3, 5)
    for i in range(len(items) + lags[-1]):
        if i < len(items):
            b = items[i]
            k = b // groups
            if pair and k not in ready:
                g_step((k, 0, 1))
                ready.add(k)
            while not pair and len(todo) > (planes - 1 - k) * plane:
                g_step(todo.pop(0))
            if pair and i == 1:
                for c in range(chunks):
                    a_copy(c).wait()
            out_dot(b)
        for step, lag in zip(steps, lags):
            if 0 <= i - lag < len(items):
                step(items[i - lag])

    for offset in offsets:
        g_each(offset, lambda copy: copy.wait_send())

    @pl.loop(0, chunks)
    def _(c):
        kv_sends(c, lambda copy: copy.wait_send())
        if relay:
            for slot, onward, valid, peer in passed:

                @pl.when(valid)
                def _(slot=slot, onward=onward, peer=peer):
                    kv_copy(slot, onward, 0, c, peer).wait_send()

    @pl.when(s == 0)
    def _():
        for b in range(groups * planes):
            s_copy(b).wait_send()

    for b in range(groups * planes):
        out_copy(b, 0).wait()
        out_copy(b, 1).wait()


def split(tiles):
    side = int(round((tiles // 4) ** 0.5))
    assert 4 * side * side == tiles
    return (4, side, side)


def body(tiles, *args):
    (
        latents,
        start,
        cached_velocity,
        shift,
        scale,
        gate,
        step_sizes,
        converged,
        neighbours,
        w_qkv,
        q_gain,
        k_gain,
        w_out,
    ) = args
    tok, width = latents.shape[1], latents.shape[2]
    group = w_qkv.shape[2]
    hd = q_gain.shape[0]
    shard = w_out.shape[1]
    dims = split(tiles)
    planes = dims[0]
    groups = 2 if dims[1] == 2 else 1
    blocks = groups * planes
    pcols = width // blocks
    cw = 2 * hd
    chunks = group // cw
    wt = w_out.T
    any_space = pl.BlockSpec(memory_space=pl.ANY)
    vmem = pl.BlockSpec(memory_space=pltpu.VMEM)
    smem = pl.BlockSpec(memory_space=pltpu.SMEM)
    dma = pltpu.SemaphoreType.DMA
    upd, vel = pl.pallas_call(
        functools.partial(kernel, tiles, dims),
        out_shape=[jax.ShapeDtypeStruct((1, tok, width), F32)] * 2,
        in_specs=[
            vmem,
            any_space,
            any_space,
            vmem,
            vmem,
            vmem,
            smem,
            smem,
            smem,
            any_space,
            vmem,
            vmem,
            any_space,
        ],
        out_specs=[any_space, any_space],
        scratch_shapes=[
            pltpu.VMEM((2, tok, width), BF16),
            pltpu.VMEM((3, chunks, width, cw), BF16),
            pltpu.VMEM((5, chunks, 2, 2 * tok, cw), BF16),
            pltpu.VMEM((chunks, 2 * tok, cw), BF16),
            pltpu.VMEM((chunks, 2, tok, cw), BF16),
            pltpu.VMEM((chunks, 2, tok, cw), BF16),
            pltpu.VMEM((2, tiles // groups, shard, group // 2), BF16),
            pltpu.VMEM((tok, width), F32),
            pltpu.VMEM((tok, width), F32),
            pltpu.VMEM((planes, groups, 2, tok, pcols), F32),
            pltpu.VMEM((planes, groups, tok, pcols), BF16),
            pltpu.VMEM((planes, groups, tok, pcols), BF16),
            pltpu.VMEM((blocks, tok, pcols), BF16),
            pltpu.VMEM((blocks, tok, pcols), BF16),
            pltpu.VMEM((planes, tok, pcols), BF16),
            pltpu.VMEM((planes, tok, pcols), BF16),
            pltpu.VMEM((blocks, tok, pcols), F32),
            pltpu.VMEM((blocks, tok, pcols), F32),
            dma((3 * chunks,)),
            dma((4,)),
            dma((2, 2)),
            dma((5, chunks)),
            dma((5, chunks)),
            dma((2, tiles // groups, 6)),
            dma((2, tiles // groups)),
            dma((2, blocks)),
            dma((2, blocks)),
            dma((2, chunks)),
            dma((2, planes)),
            dma((2, blocks)),
        ],
        compiler_params=pltpu.CompilerParams(
            collective_id=0, has_side_effects=True, vmem_limit_bytes=60 * 1024 * 1024
        ),
    )(
        latents,
        start,
        cached_velocity,
        shift,
        scale,
        gate,
        step_sizes,
        converged.T,
        neighbours,
        w_qkv,
        q_gain[None],
        k_gain[None],
        wt,
    )
    return (upd, vel)


def solution(mesh):
    assert mesh.shape["step"] == 2
    placed = (
        P("step", "tile", None),
        P("tile", None),
        P("step", "tile", None),
        P("step", None),
        P("step", None),
        P("step", None),
        P("step"),
        P(None, "tile"),
        P("tile", None),
        P(None, None, "step"),
        P(),
        P(),
        P("step", "tile"),
    )
    return jax.shard_map(
        functools.partial(body, mesh.shape["tile"]),
        mesh=mesh,
        in_specs=placed,
        out_specs=(P("step", "tile", None), P("step", "tile", None)),
        check_vma=False,
    )
```
